32 devices in a mesh: dp: 8 (over y, x, core), seq: 4 (over z).
Axes of the slice: x: 2, y: 2, z: 4, core: 2. Of those that a mesh axis runs over, the one named last changes fastest.
Arguments:
- block_input: bfloat16 [4096, 1024], P(('dp', 'seq')), may hold values from -6 to 6
- cotangent: bfloat16 [4096, 1024], P(('dp', 'seq')), may hold values from -6 to 6
- ln1_gain: bfloat16 [1024], P(('dp', 'seq')), may hold values from 0.5 to 1.5
- ln1_bias: bfloat16 [1024], P(('dp', 'seq')), may hold values from -3 to 3
- qkv_weight: bfloat16 [1024, 3072], P(('dp', 'seq')), may hold values from -0.25 to 0.25
- qv_bias: bfloat16 [2048], P(('dp', 'seq')), may hold values from -3 to 3
- out_weight: bfloat16 [1024, 1024], P(('dp', 'seq')), may hold values from -0.75 to 0.75
- out_bias: bfloat16 [1024], P(('dp', 'seq')), may hold values from -3 to 3
- ln2_gain: bfloat16 [1024], P(('dp', 'seq')), may hold values from 0.5 to 1.5
- ln2_bias: bfloat16 [1024], P(('dp', 'seq')), may hold values from -3 to 3
- fc_weight: bfloat16 [1024, 4096], P(('dp', 'seq')), may hold values from -0.1875 to 0.1875
- fc_bias: bfloat16 [4096], P(('dp', 'seq')), may hold values from -3 to 3
- proj_weight: bfloat16 [4096, 1024], P(('dp', 'seq')), may hold values from -0.09375 to 0.09375
- proj_bias: bfloat16 [1024], P(('dp', 'seq')), may hold values from -3 to 3
Outputs:
- block_output: float32 [4096, 1024], P(('dp', 'seq'))
- grad_input: float32 [4096, 1024], P(('dp', 'seq'))
- grad_ln1_gain: float32 [1024], P(('dp', 'seq'))
- grad_ln1_bias: float32 [1024], P(('dp', 'seq'))
- grad_qkv_weight: float32 [1024, 3072], P(('dp', 'seq'))
- grad_qv_bias: float32 [2048], P(('dp', 'seq'))
- grad_out_weight: float32 [1024, 1024], P(('dp', 'seq'))
- grad_out_bias: float32 [1024], P(('dp', 'seq'))
- grad_ln2_gain: float32 [1024], P(('dp', 'seq'))
- grad_ln2_bias: float32 [1024], P(('dp', 'seq'))
- grad_fc_weight: float32 [1024, 4096], P(('dp', 'seq'))
- grad_fc_bias: float32 [4096], P(('dp', 'seq'))
- grad_proj_weight: float32 [4096, 1024], P(('dp', 'seq'))
- grad_proj_bias: float32 [1024], P(('dp', 'seq'))
The draws below stay inside these ranges and needn't reach their ends.
All inputs are finite; a program needn't handle non-finite values.
Results may differ from the reference program's by a relative error of at most 0.02.
Values may be sent and summed in bfloat16 or wider, within the bound.
A program may use at most 192 MiB of HBM per device.

```python
import math
import jax
import jax.numpy as jnp
from jax import lax

D = 1024
H = 16
HD = 64
FF = 4096
SEQ_LEN = 512
SEQS = 8
TOKENS = 4096


def draw_cotangent(key, part):
    rising = 0.5 + jnp.arange(TOKENS, dtype=jnp.float32) / TOKENS
    base_draw = jax.random.truncated_normal(key, -4.0, 4.0, (TOKENS, D), jnp.float32)
    return (base_draw * rising[:, None]).astype(jnp.bfloat16)


def block_scale(key, shape, split, least, top_value):
    def one(axis_at, shards_of):
        draws = jax.random.uniform(jax.random.fold_in(jax.random.fold_in(key, 6), axis_at), (shards_of,), jnp.float32, least / len(split), top_value / len(split))
        return jnp.repeat(jnp.exp(draws), shape[axis_at] // shards_of).reshape((-1,) + (1,) * (len(shape) - axis_at - 1))

    loudness = one(*split[0])
    for cut in split[1:]:
        loudness = loudness * one(*cut)
    return loudness


def gaussian(own_key, dims, deviation, reach, cuts=(), kind=jnp.bfloat16):
    loudness = block_scale(own_key, dims, cuts, -0.22, 0.18) if cuts else 1.0
    values = jax.random.normal(own_key, dims, jnp.float32) * deviation * loudness
    return jnp.minimum(jnp.maximum(values, -reach), reach).astype(kind)


def setup_inputs(seed: int = 0) -> dict:
    arg_keys = jax.random.split(jax.random.key(seed), 15)
    block_input = gaussian(arg_keys[0], (TOKENS, D), 1.0, 6.0, ((0, 32),))
    cotangent = draw_cotangent(jax.random.fold_in(arg_keys[14], 71), 0)
    ln1_gain = jnp.clip(1.0 + 0.1 * jax.random.normal(arg_keys[2], (D,), jnp.float32), 0.5, 1.5).astype(jnp.bfloat16)
    ln1_bias = gaussian(arg_keys[3], (D,), 0.5, 3.0, ((0, 32),))
    qkv_weight = gaussian(arg_keys[4], (D, 3 * D), (D // 2) ** -0.5, 0.25, ((0, 32),))
    qv_bias = gaussian(arg_keys[5], (2 * D,), 0.5, 3.0, ((0, 32),))
    out_weight = gaussian(arg_keys[6], (D, D), (D // 16) ** -0.5, 0.75, ((0, 32),))
    out_bias = gaussian(arg_keys[7], (D,), 0.5, 3.0, ((0, 32),))
    ln2_gain = jnp.clip(1.0 + 0.1 * jax.random.normal(arg_keys[8], (D,), jnp.float32), 0.5, 1.5).astype(jnp.bfloat16)
    ln2_bias = gaussian(arg_keys[9], (D,), 0.5, 3.0, ((0, 32),))
    fc_weight = gaussian(arg_keys[10], (D, FF), D ** -0.5, 0.1875, ((0, 32),))
    fc_bias = gaussian(arg_keys[11], (FF,), 0.5, 3.0, ((0, 32),))
    proj_weight = gaussian(arg_keys[12], (FF, D), FF ** -0.5, 0.09375, ((0, 32),))
    proj_bias = gaussian(arg_keys[13], (D,), 0.5, 3.0, ((0, 32),))
    return {"block_input": block_input, "cotangent": cotangent, "ln1_gain": ln1_gain, "ln1_bias": ln1_bias, "qkv_weight": qkv_weight, "qv_bias": qv_bias, "out_weight": out_weight, "out_bias": out_bias, "ln2_gain": ln2_gain, "ln2_bias": ln2_bias, "fc_weight": fc_weight, "fc_bias": fc_bias, "proj_weight": proj_weight, "proj_bias": proj_bias}


EPS = 1e-05
GELU_COEF = math.sqrt(2.0 / math.pi)

def layer_norm(values, norm_gain, offset):
    center = lax.optimization_barrier(jnp.mean(values, axis=-1, keepdims=True))
    centred = values - center
    spread = lax.optimization_barrier(jnp.mean(centred * centred, axis=-1, keepdims=True))
    return centred * lax.rsqrt(spread + EPS) * norm_gain + offset

def gelu_tanh(pre_act):
    return 0.5 * pre_act * (1.0 + jnp.tanh(GELU_COEF * (pre_act + 0.044715 * pre_act * pre_act * pre_act)))

def halved(values):
    return values.astype(jnp.bfloat16)

def widened(values):
    return values.astype(jnp.float32)

def matmul(left, right):
    return jnp.dot(left, right, preferred_element_type=jnp.float32)

def run_sequence(inputs, upstream, params):
    ln1_gain, ln1_bias, qkv_weight, qv_bias, out_weight, out_bias, ln2_gain, ln2_bias, fc_weight, fc_bias, proj_weight, proj_bias = params
    length = inputs.shape[0]
    score_scale = HD ** (-0.5)
    gain_one = widened(ln1_gain)
    bias_one = widened(ln1_bias)
    gain_two = widened(ln2_gain)
    bias_two = widened(ln2_bias)
    stream = widened(inputs)
    normed_one = halved(layer_norm(stream, gain_one, bias_one))
    projected = matmul(normed_one, qkv_weight)
    queries = halved(projected[:, :D] + widened(qv_bias[:D]))
    key_rows = halved(projected[:, D:2 * D])
    value_rows = halved(projected[:, 2 * D:] + widened(qv_bias[D:]))
    query_heads = widened(queries).reshape(length, H, HD)
    key_heads = widened(key_rows).reshape(length, H, HD)
    value_heads = widened(value_rows).reshape(length, H, HD)
    causal = jnp.tril(jnp.ones((length, length), dtype=bool))
    scores = jnp.einsum('qhd,khd->hqk', query_heads, key_heads) * score_scale
    row_total = lax.optimization_barrier(jnp.sum(jnp.where(causal, jnp.exp(scores), 0.0), axis=-1))
    log_total = jnp.log(row_total)
    shares = jnp.where(causal, jnp.exp(scores - log_total[:, :, None]), 0.0)
    shares_half = widened(halved(shares))
    attended = halved(jnp.einsum('hqk,khd->qhd', shares_half, value_heads).reshape(length, D))
    middle = stream + matmul(attended, out_weight) + widened(out_bias)
    normed_two = halved(layer_norm(middle, gain_two, bias_two))
    pre_act = matmul(normed_two, fc_weight) + widened(fc_bias)
    hidden = halved(gelu_tanh(pre_act))
    output = middle + matmul(hidden, proj_weight) + widened(proj_bias)
    grad_out = widened(upstream)
    grad_half = halved(grad_out)
    d_proj_weight = matmul(hidden.T, grad_half)
    d_proj_bias = lax.optimization_barrier(jnp.sum(grad_out, axis=0))
    grad_hidden = matmul(grad_half, proj_weight.T)
    _, gelu_back = jax.vjp(gelu_tanh, pre_act)
    grad_pre = gelu_back(grad_hidden)[0]
    pre_half = halved(grad_pre)
    d_fc_weight = matmul(normed_two.T, pre_half)
    d_fc_bias = lax.optimization_barrier(jnp.sum(grad_pre, axis=0))
    grad_normed_two = matmul(pre_half, fc_weight.T)
    _, norm_back_two = jax.vjp(layer_norm, middle, gain_two, bias_two)
    mid_branch, d_ln2_gain, d_ln2_bias = norm_back_two(grad_normed_two)
    grad_middle = grad_out + mid_branch
    middle_half = halved(grad_middle)
    d_out_weight = matmul(attended.T, middle_half)
    d_out_bias = lax.optimization_barrier(jnp.sum(grad_middle, axis=0))
    grad_attended = matmul(middle_half, out_weight.T)
    row_delta = jnp.einsum('qhd,qhd->hq', grad_attended.reshape(length, H, HD), widened(attended).reshape(length, H, HD))
    attended_grad_half = widened(halved(grad_attended)).reshape(length, H, HD)
    grad_shares = jnp.einsum('qhd,khd->hqk', attended_grad_half, value_heads)
    grad_scores = widened(halved(shares * (grad_shares - row_delta[:, :, None])))
    grad_queries = jnp.einsum('hqk,khd->qhd', grad_scores, key_heads).reshape(length, D) * score_scale
    grad_keys = jnp.einsum('hqk,qhd->khd', grad_scores, query_heads).reshape(length, D) * score_scale
    grad_values = jnp.einsum('hqk,qhd->khd', shares_half, attended_grad_half).reshape(length, D)
    grad_qkv = jnp.concatenate([grad_queries, grad_keys, grad_values], axis=1)
    qkv_half = halved(grad_qkv)
    d_qkv_weight = matmul(normed_one.T, qkv_half)
    d_qv_bias = jnp.concatenate([lax.optimization_barrier(jnp.sum(grad_queries, axis=0)), lax.optimization_barrier(jnp.sum(grad_values, axis=0))])
    grad_normed_one = matmul(qkv_half, qkv_weight.T)
    _, norm_back_one = jax.vjp(layer_norm, stream, gain_one, bias_one)
    stream_branch, d_ln1_gain, d_ln1_bias = norm_back_one(grad_normed_one)
    grad_stream = grad_middle + stream_branch
    grads = (d_ln1_gain, d_ln1_bias, d_qkv_weight, d_qv_bias, d_out_weight, d_out_bias, d_ln2_gain, d_ln2_bias, d_fc_weight, d_fc_bias, d_proj_weight, d_proj_bias)
    return (output, grad_stream, grads)

def reference(block_input, cotangent, ln1_gain, ln1_bias, qkv_weight, qv_bias, out_weight, out_bias, ln2_gain, ln2_bias, fc_weight, fc_bias, proj_weight, proj_bias):
    params = (ln1_gain, ln1_bias, qkv_weight, qv_bias, out_weight, out_bias, ln2_gain, ln2_bias, fc_weight, fc_bias, proj_weight, proj_bias)
    inputs_all = block_input.reshape(SEQS, SEQ_LEN, D)
    upstream_all = cotangent.reshape(SEQS, SEQ_LEN, D)
    zero_grads = tuple((jnp.zeros(param.shape, jnp.float32) for param in params))

    def one_sequence(carry, operands):
        output, grad_stream, grads = run_sequence(operands[0], operands[1], params)
        summed = tuple((acc + part_grad for acc, part_grad in zip(carry, grads)))
        return (summed, (output, grad_stream))
    sums, (outputs, grad_streams) = lax.scan(one_sequence, zero_grads, (inputs_all, upstream_all))
    return (outputs.reshape(TOKENS, D), grad_streams.reshape(TOKENS, D), sums[0], sums[1], sums[2], sums[3], sums[4], sums[5], sums[6], sums[7], sums[8], sums[9], sums[10], sums[11])
```

```python
import math

import jax
import jax.numpy as jnp
from jax import lax
from jax.experimental import pallas as pl
from jax.experimental.pallas import tpu as pltpu
from jax.sharding import PartitionSpec as P

D = 1024
H = 16
HD = 64
FF = 4096


EPS = 1e-05
GELU_COEF = math.sqrt(2.0 / math.pi)
MESH = pl.DeviceIdType.MESH


def layer_norm(values, norm_gain, offset):
    center = jnp.mean(values, axis=-1, keepdims=True)
    centred = values - center
    spread = jnp.mean(centred * centred, axis=-1, keepdims=True)
    return centred * lax.rsqrt(spread + EPS) * norm_gain + offset


def gelu_tanh(pre_act):
    return (
        0.5
        * pre_act
        * (1.0 + jnp.tanh(GELU_COEF * (pre_act + 0.044715 * pre_act * pre_act * pre_act)))
    )


def halved(values):
    return values.astype(jnp.bfloat16)


def widened(values):
    return values.astype(jnp.float32)


def matmul(left, right):
    return jnp.dot(left, right, preferred_element_type=jnp.float32)


def place():
    return lax.axis_index("dp"), lax.axis_index("seq")


def counts():
    return lax.axis_size("dp"), lax.axis_size("seq")


def remote(src, dst, send, recv, device):
    return pltpu.make_async_remote_copy(
        src_ref=src, dst_ref=dst, send_sem=send, recv_sem=recv, device_id=device, device_id_type=MESH
    )


def dma(*shape):
    return pltpu.SemaphoreType.DMA(shape)


def greet_all():
    dp, s = place()
    dpc, n = counts()
    barrier = pltpu.get_barrier_semaphore()

    def greet(i, carry):
        @pl.when(i != dp * n + s)
        def _():
            pl.semaphore_signal(barrier, inc=1, device_id=(i // n, i % n), device_id_type=MESH)

        return carry

    lax.fori_loop(0, dpc * n, greet, 0)
    pl.semaphore_wait(barrier, dpc * n - 1)


def greet_near():
    dp, s = place()
    dpc, n = counts()
    nc = dpc // 2
    barrier = pltpu.get_barrier_semaphore()
    for k in range(1, n):
        pl.semaphore_signal(barrier, inc=1, device_id=(dp, (s + k) % n), device_id_type=MESH)
    for k in range(1, nc):
        pl.semaphore_signal(barrier, inc=1, device_id=((dp + 2 * k) % dpc, s), device_id_type=MESH)
    pl.semaphore_signal(barrier, inc=1, device_id=(other_core(dp), s), device_id_type=MESH)
    pl.semaphore_wait(barrier, n - 1 + nc)


def greet_seq():
    dp, s = place()
    _, n = counts()
    barrier = pltpu.get_barrier_semaphore()
    for k in range(1, n):
        pl.semaphore_signal(barrier, inc=1, device_id=(dp, (s + k) % n), device_id_type=MESH)
    pl.semaphore_wait(barrier, n - 1)


def other_core(dp):
    return dp + 1 - 2 * (dp % 2)


class Exchange:
    def __init__(self, value):
        _, n = counts()
        self.operands = (value,)
        self.outs = (value,)
        self.sems = (dma(n), dma(n))

    def copies(self, ins, outs, sems):
        dp, s = place()
        _, n = counts()
        return [
            remote(
                ins[0].at[(s + k) % n], outs[0].at[s], sems[0].at[k], sems[1].at[k], (dp, (s + k) % n)
            )
            for k in range(n - 1, 0, -1)
        ]

    def start(self, ins, outs, sems):
        for copy in self.copies(ins, outs, sems):
            copy.start()

    def finish(self, ins, outs, sems):
        for copy in self.copies(ins, outs, sems):
            copy.wait()


class Plane(Exchange):
    def __init__(self, value):
        dpc, _ = counts()
        self.operands = (value,)
        self.outs = (value,)
        self.sems = (dma(dpc // 2), dma(dpc // 2))

    def copies(self, ins, outs, sems):
        dp, s = place()
        dpc, _ = counts()
        chip, core, nc = dp // 2, dp % 2, dpc // 2
        return [
            remote(
                ins[0].at[(chip + k) % nc],
                outs[0].at[chip],
                sems[0].at[k],
                sems[1].at[k],
                ((chip + k) % nc * 2 + core, s),
            )
            for k in range(1, nc)
        ]


class Partner(Exchange):
    def __init__(self, value):
        self.operands = (value,)
        self.outs = (jax.ShapeDtypeStruct(value.shape[1:], value.dtype),)
        self.sems = (dma(1), dma(1))

    def copies(self, ins, outs, sems):
        dp, s = place()
        return [
            remote(
                ins[0].at[1 - dp % 2], outs[0], sems[0].at[0], sems[1].at[0], (other_core(dp), s)
            )
        ]


class Everyone:
    def __init__(self, value):
        dpc, n = counts()
        self.operands = (value,)
        self.outs = (value,)
        self.sems = (dma(dpc * n), dma(dpc * n))

    def copy(self, ins, outs, sems, k):
        dp, s = place()
        dpc, n = counts()
        me = dp * n + s
        peer = (me + k) % (dpc * n)
        return remote(
            ins[0].at[peer], outs[0].at[me], sems[0].at[k], sems[1].at[k], (peer // n, peer % n)
        )

    def start(self, ins, outs, sems):
        def step(k, carry):
            self.copy(ins, outs, sems, k).start()
            return carry

        lax.fori_loop(1, self.outs[0].shape[0], step, 0)

    def finish(self, ins, outs, sems):
        def step(k, carry):
            self.copy(ins, outs, sems, k).wait()
            return carry

        lax.fori_loop(1, self.outs[0].shape[0], step, 0)


class Line:
    def __init__(self, value):
        _, n = counts()
        self.operands = (value,)
        self.outs = (jax.ShapeDtypeStruct((n,) + value.shape, value.dtype),)
        self.sems = (dma(2, n), dma(2, n), dma(1))

    def hand_on(self, ins, outs, sems, way, k):
        dp, s = place()
        sign = 1 - 2 * way
        block = outs[0].at[s - sign * k]
        return remote(
            ins[0] if k == 0 else block, block, sems[0].at[way, k], sems[1].at[way, k], (dp, s + sign)
        )

    def guard(self, way, k):
        _, s = place()
        _, n = counts()
        return (s >= k) if way == 0 else (s < n - k)

    def start(self, ins, outs, sems):
        _, s = place()
        _, n = counts()
        pltpu.make_async_copy(ins[0], outs[0].at[s], sems[2].at[0]).start()
        for way in (0, 1):
            follows = (s < n - 1) if way == 0 else (s > 0)

            @pl.when(follows)
            def _():
                self.hand_on(ins, outs, sems, way, 0).start()

    def step(self, ins, outs, sems, k):
        dp, s = place()
        _, n = counts()
        for way in (0, 1):
            sign = 1 - 2 * way
            follows = (s < n - 1) if way == 0 else (s > 0)

            @pl.when(self.guard(way, k))
            def _():
                block = outs[0].at[s - sign * k]
                remote(
                    block, block, sems[0].at[way, k - 1], sems[1].at[way, k - 1], (dp, s - sign)
                ).wait_recv()
                if k < n - 1:

                    @pl.when(follows)
                    def _():
                        self.hand_on(ins, outs, sems, way, k).start()

    def close(self, ins, outs, sems):
        _, s = place()
        _, n = counts()
        for way in (0, 1):
            follows = (s < n - 1) if way == 0 else (s > 0)
            for k in range(n - 1):

                @pl.when(jnp.logical_and(follows, self.guard(way, k)))
                def _():
                    self.hand_on(ins, outs, sems, way, k).wait_send()

        pltpu.make_async_copy(ins[0], outs[0].at[s], sems[2].at[0]).wait()

    def finish(self, ins, outs, sems):
        _, n = counts()
        for k in range(1, n):
            self.step(ins, outs, sems, k)
        self.close(ins, outs, sems)


class Turn:
    def __init__(self, value, outward):
        self.outward = outward
        self.operands = (value,)
        self.outs = (value,)
        self.sems = (dma(1), dma(1), dma(1))

    def target(self):
        dp, s = place()
        dpc, n = counts()
        if self.outward:
            rank = s * dpc + dp
            return rank // n, rank % n
        rank = dp * n + s
        return rank % dpc, rank // dpc

    def away(self):
        dp, s = place()
        to_dp, to_s = self.target()
        return jnp.logical_or(to_dp != dp, to_s != s)

    def copy(self, ins, outs, sems):
        return remote(ins[0], outs[0], sems[0].at[0], sems[1].at[0], self.target())

    def start(self, ins, outs, sems):
        @pl.when(self.away())
        def _():
            self.copy(ins, outs, sems).start()

        @pl.when(jnp.logical_not(self.away()))
        def _():
            pltpu.make_async_copy(ins[0], outs[0], sems[2].at[0]).start()

    def finish(self, ins, outs, sems):
        @pl.when(self.away())
        def _():
            self.copy(ins, outs, sems).wait()

        @pl.when(jnp.logical_not(self.away()))
        def _():
            pltpu.make_async_copy(ins[0], outs[0], sems[2].at[0]).wait()


def run(number, greet, *tasks):
    spans = []
    a = b = c = 0
    for task in tasks:
        spans.append((a, b, c))
        a += len(task.operands)
        b += len(task.outs)
        c += len(task.sems)
    n_in, n_out = a, b

    def kernel(*refs):
        ins, outs, sems = refs[:n_in], refs[n_in : n_in + n_out], refs[n_in + n_out :]
        greet()
        views = [
            (
                ins[i : i + len(t.operands)],
                outs[o : o + len(t.outs)],
                sems[m : m + len(t.sems)],
            )
            for t, (i, o, m) in zip(tasks, spans)
        ]
        for t, view in zip(tasks, views):
            t.start(*view)
        for t, view in zip(tasks, views):
            t.finish(*view)

    return pl.pallas_call(
        kernel,
        out_shape=[jax.ShapeDtypeStruct(o.shape, o.dtype) for t in tasks for o in t.outs],
        in_specs=[pl.BlockSpec(memory_space=pl.ANY)] * n_in,
        out_specs=[pl.BlockSpec(memory_space=pl.ANY)] * n_out,
        scratch_shapes=[s for t in tasks for s in t.sems],
        compiler_params=pltpu.CompilerParams(collective_id=number, has_side_effects=True),
    )(*[v for t in tasks for v in t.operands])


def gather_inputs(block_input, cotangent, pack, out_rows, proj_rows):
    dpc, n = counts()
    nc = dpc // 2
    tokens, grads = Line(block_input), Line(cotangent)

    def kernel(
        x_in, g_in, pack_in, out_in, proj_in, x_all, g_all, pack_all, out_all, proj_all,
        x_send, x_recv, x_own, g_send, g_recv, g_own, turn_send, turn_recv, local,
        z_send, z_recv, c_send, c_recv, p_send, p_recv,
    ):
        dp, s = place()
        chip, core = dp // 2, dp % 2
        greet_all()
        gathered = (proj_all, out_all, pack_all)
        rank = dp * n + s
        to_dp, to_s = rank % dpc, rank // dpc
        home = jnp.logical_and(to_dp == dp, to_s == s)
        turn = remote(
            out_in, out_all.at[to_dp], turn_send.at[0], turn_recv.at[0], (to_dp, to_s)
        )
        keep_out = pltpu.make_async_copy(out_in, out_all.at[dp], local.at[1])
        keep_pack = pltpu.make_async_copy(pack_in.at[s], pack_all.at[dp, s], local.at[2])
        keep_proj = pltpu.make_async_copy(proj_in, proj_all.at[dp], local.at[0])
        keep_pack.start()
        shuffles = [
            remote(
                pack_in.at[(s + k) % n], pack_all.at[dp, s], z_send.at[k], z_recv.at[k],
                (dp, (s + k) % n),
            )
            for k in range(n - 1, 0, -1)
        ]
        for copy in shuffles:
            copy.start()

        @pl.when(home)
        def _():
            keep_out.start()

        @pl.when(jnp.logical_not(home))
        def _():
            turn.start()

        keep_proj.start()

        def to_chips(a, source):
            return [
                remote(
                    source, gathered[a].at[dp], c_send.at[a, k], c_recv.at[a, k],
                    ((chip + k) % nc * 2 + core, s),
                )
                for k in range(1, nc)
            ]

        def to_partner(a, k, source):
            slot = (chip - k + nc) % nc * 2 + core
            return remote(
                source if source is not None else gathered[a].at[slot],
                gathered[a].at[slot], p_send.at[a, k], p_recv.at[a, k], (other_core(dp), s),
            )

        def arrive(a, k):
            block = gathered[a].at[(chip - k + nc) % nc * 2 + core]
            remote(
                block, block, c_send.at[a, k], c_recv.at[a, k], ((chip - k + nc) % nc * 2 + core, s)
            ).wait_recv()

        sources = (proj_in, out_all.at[dp], pack_all.at[dp])
        tokens.start((x_in,), (x_all,), (x_send, x_recv, x_own))
        for copy in to_chips(0, sources[0]):
            copy.start()
        to_partner(0, 0, sources[0]).start()

        @pl.when(home)
        def _():
            keep_out.wait()

        @pl.when(jnp.logical_not(home))
        def _():
            turn.wait()

        keep_pack.wait()
        for copy in shuffles:
            copy.wait()
        for a in (1, 2):
            for copy in to_chips(a, sources[a]):
                copy.start()
            to_partner(a, 0, sources[a]).start()
        for k in range(1, n):
            tokens.step((x_in,), (x_all,), (x_send, x_recv, x_own), k)
            if k == 1:
                grads.start((g_in,), (g_all,), (g_send, g_recv, g_own))
        for a in range(3):
            for k in range(1, nc):
                arrive(a, k)
                to_partner(a, k, None).start()
        for k in range(1, n):
            grads.step((g_in,), (g_all,), (g_send, g_recv, g_own), k)
        tokens.close((x_in,), (x_all,), (x_send, x_recv, x_own))
        grads.close((g_in,), (g_all,), (g_send, g_recv, g_own))
        for a in range(3):
            for copy in to_chips(a, sources[a]):
                copy.wait_send()
            for k in range(nc):
                slot = (chip - k + nc) % nc * 2 + 1 - core
                to_partner(a, k, sources[a] if k == 0 else None).wait_send()
                block = gathered[a].at[slot]
                remote(
                    block, block, p_send.at[a, k], p_recv.at[a, k], (other_core(dp), s)
                ).wait_recv()
        keep_proj.wait()

    def grown(value, *lead):
        return jax.ShapeDtypeStruct(lead + value.shape, value.dtype)

    return pl.pallas_call(
        kernel,
        out_shape=[
            grown(block_input, n), grown(cotangent, n), grown(pack, dpc), grown(out_rows, dpc),
            grown(proj_rows, dpc),
        ],
        in_specs=[pl.BlockSpec(memory_space=pl.ANY)] * 5,
        out_specs=[pl.BlockSpec(memory_space=pl.ANY)] * 5,
        scratch_shapes=[
            *tokens.sems, *grads.sems, dma(1), dma(1), dma(3),
            dma(n), dma(n), dma(3, nc), dma(3, nc), dma(3, nc), dma(3, nc),
        ],
        compiler_params=pltpu.CompilerParams(collective_id=0, has_side_effects=True),
    )(block_input, cotangent, pack, out_rows, proj_rows)


def total(own, received, mine):
    picked = [
        jnp.where(k == mine, widened(own[k]), widened(received[k])) for k in range(own.shape[0])
    ]
    result = picked[0]
    for value in picked[1:]:
        result = result + value
    return result


def fill(own, received, mine):
    slots = lax.broadcasted_iota(jnp.int32, (own.shape[0],) + (1,) * (own.ndim - 1), 0)
    return jnp.where(slots == mine, own, received)


def local(
    block_input,
    cotangent,
    ln1_gain,
    ln1_bias,
    qkv_weight,
    qv_bias,
    out_weight,
    out_bias,
    ln2_gain,
    ln2_bias,
    fc_weight,
    fc_bias,
    proj_weight,
    proj_bias,
):
    dp, s = place()
    dpc, n = counts()
    nc, ranks = dpc // 2, dpc * n
    core, chip = dp % 2, dp // 2
    tok_rows = block_input.shape[0]
    rows = qkv_weight.shape[0]
    units = fc_bias.shape[0]
    heads = H // n
    wide = heads * HD
    length = n * tok_rows
    score_scale = HD ** (-0.5)

    small = jnp.concatenate(
        [ln1_gain, ln1_bias, out_bias, ln2_gain, ln2_bias, proj_bias, qv_bias, fc_bias]
    )
    margin = -(-small.shape[0] // (rows * 128)) * 128
    block = jnp.pad(small, (0, rows * margin - small.shape[0])).reshape(rows, margin)
    pack = jnp.concatenate(
        [
            qkv_weight.reshape(rows, 3, n, wide).transpose(2, 0, 1, 3).reshape(n, rows, 3 * wide),
            fc_weight.reshape(rows, dpc, n, units).transpose(2, 0, 1, 3).reshape(n, rows, dpc * units),
            jnp.broadcast_to(block[None], (n, rows, margin)),
        ],
        axis=2,
    )
    x_all, g_all, pack_all, out_all, proj_all = gather_inputs(
        block_input, cotangent, pack, out_weight, proj_weight
    )
    stream_seq = widened(x_all.reshape(length, D))
    grad_seq = g_all.reshape(length, D)
    pack_rows = pack_all.reshape(D, pack.shape[2])
    qkv_cols = pack_rows[:, : 3 * wide]
    fc_cols = pack_rows[:, 3 * wide : 3 * wide + dpc * units]
    out_rows = out_all.reshape(wide, D)
    proj_rows = proj_all.reshape(dpc * units, D)
    smalls = pack_rows[:, 3 * wide + dpc * units :].reshape(ranks, rows * margin)
    gain_one, bias_one, out_bias_full, gain_two, bias_two, proj_bias_full = (
        widened(smalls[:, i * rows : (i + 1) * rows].reshape(D)) for i in range(6)
    )
    at = 6 * rows
    qv_full = smalls[:, at : at + qv_bias.shape[0]].reshape(2, n, wide)
    qv_own = widened(lax.dynamic_index_in_dim(qv_full, s, 1, keepdims=False))
    at += qv_bias.shape[0]
    fc_bias_cols = widened(
        lax.dynamic_index_in_dim(
            smalls[:, at : at + units].reshape(dpc, n, units), s, 1, keepdims=False
        ).reshape(dpc * units)
    )

    normed_one = halved(layer_norm(stream_seq, gain_one, bias_one))
    projected = matmul(normed_one, qkv_cols)

    def by_head(values):
        return values.reshape(length, heads, HD).transpose(1, 0, 2)

    def by_token(values):
        return values.transpose(1, 0, 2).reshape(length, wide)

    queries = by_head(halved(projected[:, :wide] + qv_own[0]))
    keys = by_head(halved(projected[:, wide : 2 * wide]))
    values = by_head(halved(projected[:, 2 * wide :] + qv_own[1]))
    position = jnp.arange(length, dtype=jnp.int32)
    visible = position[None, :] <= position[:, None]
    scores = (
        jnp.einsum("hqd,hkd->hqk", queries, keys, preferred_element_type=jnp.float32) * score_scale
    )
    log_total = jnp.log(
        jnp.sum(jnp.where(visible, jnp.exp(scores), 0.0), axis=-1, keepdims=True)
    )
    probs = jnp.where(visible, jnp.exp(scores - log_total), 0.0)
    shares = halved(probs)
    attended_heads = halved(
        jnp.einsum("hqk,hkd->hqd", shares, values, preferred_element_type=jnp.float32)
    )
    attended = by_token(attended_heads)
    mixed = halved(matmul(attended, out_rows)).reshape(n, tok_rows, D)
    (mixed_got,) = run(1, greet_seq, Exchange(mixed))
    stream = widened(block_input)
    middle = stream + total(mixed, mixed_got, s) + out_bias_full
    normed_two = halved(layer_norm(middle, gain_two, bias_two))
    (normed_all,) = run(2, greet_seq, Line(normed_two))
    normed_seq = normed_all.reshape(length, D)
    grad_out = widened(cotangent)
    d_proj_bias = jnp.sum(grad_out, axis=0)
    pre_act = matmul(normed_seq, fc_cols) + fc_bias_cols
    hidden = halved(gelu_tanh(pre_act))
    grad_hidden = matmul(grad_seq, proj_rows.T)
    _, gelu_back = jax.vjp(gelu_tanh, pre_act)
    grad_pre = gelu_back(grad_hidden)[0]
    pre_half = halved(grad_pre)
    back_two = halved(matmul(pre_half, fc_cols.T)).reshape(n, tok_rows, D)
    (back_two_got,) = run(3, greet_seq, Exchange(back_two))
    ff_part = halved(matmul(hidden, proj_rows)).reshape(n, tok_rows, D)

    def by_core(values):
        return halved(values).reshape(nc, 2, -1, values.shape[-1]).transpose(1, 0, 2, 3)

    d_proj = by_core(matmul(hidden.T, grad_seq))
    d_fc = by_core(matmul(normed_seq.T, pre_half))
    d_fc_bias = jnp.sum(grad_pre, axis=0).reshape(dpc, 1, units)
    _, norm_back_two = jax.vjp(layer_norm, middle, gain_two, bias_two)
    mid_branch, d_ln2_gain, d_ln2_bias = norm_back_two(total(back_two, back_two_got, s))
    grad_middle = grad_out + mid_branch
    d_out_bias = jnp.sum(grad_middle, axis=0)
    middle_all, d_proj_got, d_fc_got = run(
        4, greet_near, Line(halved(grad_middle)), Partner(d_proj), Partner(d_fc)
    )

    def pair(own, received):
        kept = lax.dynamic_index_in_dim(own, core, 0, keepdims=False)
        return halved(widened(kept) + widened(received))

    d_proj, d_fc = pair(d_proj, d_proj_got), pair(d_fc, d_fc_got)
    middle_half = middle_all.reshape(length, D)
    d_out = by_core(matmul(attended.T, middle_half))
    grad_attended = matmul(middle_half, out_rows.T)
    grad_att = by_head(halved(grad_attended))
    row_delta = jnp.sum(by_head(grad_attended) * widened(attended_heads), axis=-1, keepdims=True)
    grad_shares = jnp.einsum("hqd,hkd->hqk", grad_att, values, preferred_element_type=jnp.float32)
    grad_scores = halved(probs * (grad_shares - row_delta))
    grad_q = (
        jnp.einsum("hqk,hkd->hqd", grad_scores, keys, preferred_element_type=jnp.float32)
        * score_scale
    )
    grad_k = (
        jnp.einsum("hqk,hqd->hkd", grad_scores, queries, preferred_element_type=jnp.float32)
        * score_scale
    )
    grad_v = jnp.einsum("hqk,hqd->hkd", shares, grad_att, preferred_element_type=jnp.float32)
    grad_qkv = jnp.concatenate([by_token(grad_q), by_token(grad_k), by_token(grad_v)], axis=1)
    qkv_half = halved(grad_qkv)
    back_one = halved(matmul(qkv_half, qkv_cols.T)).reshape(n, tok_rows, D)
    d_qkv = by_core(matmul(normed_one.T, qkv_half))
    sums = jnp.sum(grad_qkv, axis=0)
    d_qv = jnp.stack([sums[:wide], sums[2 * wide :]])[:, None]
    back_one_got, d_proj_parts, d_fc_parts, d_qkv_got, d_out_got = run(
        5, greet_near, Exchange(back_one), Plane(d_proj), Plane(d_fc), Partner(d_qkv), Partner(d_out)
    )
    proj_grad = total(d_proj, d_proj_parts, chip)
    fc_rows = halved(total(d_fc, d_fc_parts, chip)).reshape(n, rows, dpc * units)
    d_qkv, d_out = pair(d_qkv, d_qkv_got), pair(d_out, d_out_got)
    _, norm_back_one = jax.vjp(layer_norm, stream, gain_one, bias_one)
    stream_branch, d_ln1_gain, d_ln1_bias = norm_back_one(total(back_one, back_one_got, s))
    grad_stream = grad_middle + stream_branch
    turn = jnp.arange(n, dtype=jnp.int32)[None, :, None] == s
    vectors = jnp.concatenate(
        [
            v.reshape(ranks, rows)
            for v in (d_ln1_gain, d_ln1_bias, d_out_bias, d_ln2_gain, d_ln2_bias, d_proj_bias)
        ]
        + [
            jnp.where(turn, d_qv, 0.0).reshape(ranks, -1),
            jnp.where(turn, d_fc_bias, 0.0).reshape(ranks, units),
        ],
        axis=1,
    )
    used = vectors.shape[1]
    vectors = jnp.pad(vectors, ((0, 0), (0, -used % 128))).reshape(ranks, -1, 128)
    d_qkv_parts, d_out_parts, fc_got, vectors_got, ff_got = run(
        6, greet_all, Plane(d_qkv), Plane(d_out), Exchange(fc_rows), Everyone(vectors), Exchange(ff_part)
    )
    output = middle + total(ff_part, ff_got, s) + proj_bias_full
    fc_grad = (
        widened(fill(fc_rows, fc_got, s))
        .reshape(n, rows, dpc, units)
        .transpose(1, 2, 0, 3)
        .reshape(rows, FF)
    )
    qkv_rows = halved(total(d_qkv, d_qkv_parts, chip)).reshape(n, rows, 3 * wide)
    out_grad_rows = halved(total(d_out, d_out_parts, chip))
    vector = jnp.sum(fill(vectors, vectors_got, dp * n + s), axis=0).reshape(-1)
    firsts = [vector[i * rows : (i + 1) * rows] for i in range(6)]
    at = 6 * rows
    qv_grad = vector[at : at + qv_bias.shape[0]]
    at += qv_bias.shape[0]
    fc_bias_grad = vector[at : at + units]
    qkv_got, out_grad = run(7, greet_all, Exchange(qkv_rows), Turn(out_grad_rows, True))
    qkv_grad = (
        widened(fill(qkv_rows, qkv_got, s))
        .reshape(n, rows, 3, wide)
        .transpose(1, 2, 0, 3)
        .reshape(rows, 3 * D)
    )
    return (
        output,
        grad_stream,
        firsts[0],
        firsts[1],
        qkv_grad,
        qv_grad,
        widened(out_grad),
        firsts[2],
        firsts[3],
        firsts[4],
        fc_grad,
        fc_bias_grad,
        proj_grad,
        firsts[5],
    )


def solution(mesh):
    in_specs = (
        P(("dp", "seq"), None),
        P(("dp", "seq"), None),
        P(("dp", "seq")),
        P(("dp", "seq")),
        P(("dp", "seq"), None),
        P(("dp", "seq")),
        P(("dp", "seq"), None),
        P(("dp", "seq")),
        P(("dp", "seq")),
        P(("dp", "seq")),
        P(("dp", "seq"), None),
        P(("dp", "seq")),
        P(("dp", "seq"), None),
        P(("dp", "seq")),
    )
    out_specs = (
        P(("dp", "seq"), None),
        P(("dp", "seq"), None),
        P(("dp", "seq")),
        P(("dp", "seq")),
        P(("dp", "seq"), None),
        P(("dp", "seq")),
        P(("dp", "seq"), None),
        P(("dp", "seq")),
        P(("dp", "seq")),
        P(("dp", "seq")),
        P(("dp", "seq"), None),
        P(("dp", "seq")),
        P(("dp", "seq"), None),
        P(("dp", "seq")),
    )
    return jax.shard_map(local, mesh=mesh, in_specs=in_specs, out_specs=out_specs, check_vma=False)
```

```python
import math

import jax
import jax.numpy as jnp
from jax import lax
from jax.experimental import pallas as pl
from jax.experimental.pallas import tpu as pltpu
from jax.sharding import PartitionSpec as P

D = 1024
H = 16
HD = 64
FF = 4096


EPS = 1e-05
GELU_COEF = math.sqrt(2.0 / math.pi)
MESH = pl.DeviceIdType.MESH


def layer_norm(values, norm_gain, offset):
    center = jnp.mean(values, axis=-1, keepdims=True)
    centred = values - center
    spread = jnp.mean(centred * centred, axis=-1, keepdims=True)
    return centred * lax.rsqrt(spread + EPS) * norm_gain + offset


def gelu_tanh(pre_act):
    return (
        0.5
        * pre_act
        * (1.0 + jnp.tanh(GELU_COEF * (pre_act + 0.044715 * pre_act * pre_act * pre_act)))
    )


def halved(values):
    return values.astype(jnp.bfloat16)


def widened(values):
    return values.astype(jnp.float32)


def matmul(left, right):
    return jnp.dot(left, right, preferred_element_type=jnp.float32)


def place():
    return lax.axis_index("dp"), lax.axis_index("seq")


def counts():
    return lax.axis_size("dp"), lax.axis_size("seq")


def remote(src, dst, send, recv, device):
    return pltpu.make_async_remote_copy(
        src_ref=src, dst_ref=dst, send_sem=send, recv_sem=recv, device_id=device, device_id_type=MESH
    )


def dma(*shape):
    return pltpu.SemaphoreType.DMA(shape)


def greet_all():
    dp, s = place()
    dpc, n = counts()
    barrier = pltpu.get_barrier_semaphore()

    def greet(i, carry):
        @pl.when(i != dp * n + s)
        def _():
            pl.semaphore_signal(barrier, inc=1, device_id=(i // n, i % n), device_id_type=MESH)

        return carry

    lax.fori_loop(0, dpc * n, greet, 0)
    pl.semaphore_wait(barrier, dpc * n - 1)


def greet_near():
    dp, s = place()
    dpc, n = counts()
    nc = dpc // 2
    barrier = pltpu.get_barrier_semaphore()
    for k in range(1, n):
        pl.semaphore_signal(barrier, inc=1, device_id=(dp, (s + k) % n), device_id_type=MESH)
    for k in range(1, nc):
        pl.semaphore_signal(barrier, inc=1, device_id=((dp + 2 * k) % dpc, s), device_id_type=MESH)
    pl.semaphore_signal(barrier, inc=1, device_id=(other_core(dp), s), device_id_type=MESH)
    pl.semaphore_wait(barrier, n - 1 + nc)


def greet_seq():
    dp, s = place()
    _, n = counts()
    barrier = pltpu.get_barrier_semaphore()
    for k in range(1, n):
        pl.semaphore_signal(barrier, inc=1, device_id=(dp, (s + k) % n), device_id_type=MESH)
    pl.semaphore_wait(barrier, n - 1)


def other_core(dp):
    return dp + 1 - 2 * (dp % 2)


class Exchange:
    def __init__(self, value):
        _, n = counts()
        self.operands = (value,)
        self.outs = (value,)
        self.sems = (dma(n), dma(n))

    def copies(self, ins, outs, sems):
        dp, s = place()
        _, n = counts()
        return [
            remote(
                ins[0].at[(s + k) % n], outs[0].at[s], sems[0].at[k], sems[1].at[k], (dp, (s + k) % n)
            )
            for k in range(n - 1, 0, -1)
        ]

    def start(self, ins, outs, sems):
        for copy in self.copies(ins, outs, sems):
            copy.start()

    def finish(self, ins, outs, sems):
        for copy in self.copies(ins, outs, sems):
            copy.wait()


class Plane(Exchange):
    def __init__(self, value):
        dpc, _ = counts()
        self.operands = (value,)
        self.outs = (value,)
        self.sems = (dma(dpc // 2), dma(dpc // 2))

    def copies(self, ins, outs, sems):
        dp, s = place()
        dpc, _ = counts()
        chip, core, nc = dp // 2, dp % 2, dpc // 2
        return [
            remote(
                ins[0].at[(chip + k) % nc],
                outs[0].at[chip],
                sems[0].at[k],
                sems[1].at[k],
                ((chip + k) % nc * 2 + core, s),
            )
            for k in range(1, nc)
        ]


class Partner(Exchange):
    def __init__(self, value):
        self.operands = (value,)
        self.outs = (jax.ShapeDtypeStruct(value.shape[:1] + value.shape[2:], value.dtype),)
        self.sems = (dma(value.shape[0]), dma(value.shape[0]))

    def copies(self, ins, outs, sems):
        dp, s = place()
        return [
            remote(
                ins[0].at[k, 1 - dp % 2], outs[0].at[k], sems[0].at[k], sems[1].at[k],
                (other_core(dp), s),
            )
            for k in range(self.outs[0].shape[0])
        ]


class Spread:
    def __init__(self, value):
        dpc, _ = counts()
        nc = dpc // 2
        self.operands = (value,)
        self.outs = (jax.ShapeDtypeStruct((dpc,) + value.shape, value.dtype),)
        self.sems = (dma(nc), dma(nc), dma(nc), dma(nc), dma(1))

    def to_chips(self, ins, outs, sems):
        dp, s = place()
        dpc, _ = counts()
        nc = dpc // 2
        return [
            remote(
                ins[0], outs[0].at[dp], sems[0].at[k], sems[1].at[k],
                ((dp // 2 + k) % nc * 2 + dp % 2, s),
            )
            for k in range(1, nc)
        ]

    def to_partner(self, ins, outs, sems, k):
        dp, s = place()
        dpc, _ = counts()
        nc = dpc // 2
        block = outs[0].at[(dp // 2 - k + nc) % nc * 2 + dp % 2]
        return remote(
            ins[0] if k == 0 else block, block, sems[2].at[k], sems[3].at[k], (other_core(dp), s)
        )

    def start(self, ins, outs, sems):
        dp, _ = place()
        for copy in self.to_chips(ins, outs, sems):
            copy.start()
        self.to_partner(ins, outs, sems, 0).start()
        pltpu.make_async_copy(ins[0], outs[0].at[dp], sems[4].at[0]).start()

    def middle(self, ins, outs, sems):
        dp, s = place()
        dpc, _ = counts()
        nc = dpc // 2
        for k in range(1, nc):
            slot = (dp // 2 - k + nc) % nc * 2 + dp % 2
            block = outs[0].at[slot]
            remote(block, block, sems[0].at[k], sems[1].at[k], (slot, s)).wait_recv()
            self.to_partner(ins, outs, sems, k).start()

    def close(self, ins, outs, sems):
        dp, s = place()
        dpc, _ = counts()
        nc = dpc // 2
        for copy in self.to_chips(ins, outs, sems):
            copy.wait_send()
        for k in range(nc):
            self.to_partner(ins, outs, sems, k).wait_send()
            block = outs[0].at[(dp // 2 - k + nc) % nc * 2 + 1 - dp % 2]
            remote(block, block, sems[2].at[k], sems[3].at[k], (other_core(dp), s)).wait_recv()
        pltpu.make_async_copy(ins[0], outs[0].at[dp], sems[4].at[0]).wait()

    def finish(self, ins, outs, sems):
        self.middle(ins, outs, sems)
        self.close(ins, outs, sems)


class Owners:
    def __init__(self, value):
        self.operands = (value,)
        self.outs = (value,)
        self.count = value.shape[0] * value.shape[1]
        self.sems = (dma(self.count), dma(self.count), dma(1))

    def copy(self, ins, outs, sems, k):
        dp, s = place()
        dpc, n = counts()
        chip, z = (dp // 2 + k // n) % (dpc // 2), (s + k % n) % n
        return remote(
            ins[0].at[chip, z], outs[0].at[dp // 2, s], sems[0].at[k], sems[1].at[k],
            (chip * 2 + dp % 2, z),
        )

    def keep(self, ins, outs, sems):
        dp, s = place()
        return pltpu.make_async_copy(ins[0].at[dp // 2, s], outs[0].at[dp // 2, s], sems[2].at[0])

    def start(self, ins, outs, sems):
        def step(k, carry):
            self.copy(ins, outs, sems, k).start()
            return carry

        lax.fori_loop(1, self.count, step, 0)
        self.keep(ins, outs, sems).start()

    def finish(self, ins, outs, sems):
        def step(k, carry):
            self.copy(ins, outs, sems, k).wait()
            return carry

        lax.fori_loop(1, self.count, step, 0)
        self.keep(ins, outs, sems).wait()


class Blocks:
    def __init__(self, value):
        self.operands = (value,)
        self.outs = (value,)
        self.sems = (dma(value.shape[0]), dma(value.shape[0]), dma(1))

    def each(self, ins, outs, sems, method):
        dp, s = place()
        dpc, n = counts()
        nc = dpc // 2
        for k in range(nc):
            chip = (dp // 2 + k) % nc
            rank = s * dpc + chip * 2 + dp % 2
            to_dp, to_s = rank // n, rank % n
            away = jnp.logical_or(to_dp != dp, to_s != s)
            source, target = ins[0].at[chip], outs[0].at[dp // 2]

            @pl.when(away)
            def _():
                getattr(remote(source, target, sems[0].at[k], sems[1].at[k], (to_dp, to_s)), method)()

            @pl.when(jnp.logical_not(away))
            def _():
                getattr(pltpu.make_async_copy(source, target, sems[2].at[0]), method)()

    def start(self, ins, outs, sems):
        self.each(ins, outs, sems, "start")

    def finish(self, ins, outs, sems):
        self.each(ins, outs, sems, "wait")


class Everyone:
    def __init__(self, value):
        dpc, n = counts()
        self.operands = (value,)
        self.outs = (value,)
        self.sems = (dma(dpc * n), dma(dpc * n))

    def copy(self, ins, outs, sems, k):
        dp, s = place()
        dpc, n = counts()
        me = dp * n + s
        peer = (me + k) % (dpc * n)
        return remote(
            ins[0].at[peer], outs[0].at[me], sems[0].at[k], sems[1].at[k], (peer // n, peer % n)
        )

    def start(self, ins, outs, sems):
        def step(k, carry):
            self.copy(ins, outs, sems, k).start()
            return carry

        lax.fori_loop(1, self.outs[0].shape[0], step, 0)

    def finish(self, ins, outs, sems):
        def step(k, carry):
            self.copy(ins, outs, sems, k).wait()
            return carry

        lax.fori_loop(1, self.outs[0].shape[0], step, 0)


class Line:
    def __init__(self, value):
        _, n = counts()
        self.operands = (value,)
        self.outs = (jax.ShapeDtypeStruct((n,) + value.shape, value.dtype),)
        self.sems = (dma(2, n), dma(2, n), dma(1))

    def hand_on(self, ins, outs, sems, way, k):
        dp, s = place()
        sign = 1 - 2 * way
        block = outs[0].at[s - sign * k]
        return remote(
            ins[0] if k == 0 else block, block, sems[0].at[way, k], sems[1].at[way, k], (dp, s + sign)
        )

    def guard(self, way, k):
        _, s = place()
        _, n = counts()
        return (s >= k) if way == 0 else (s < n - k)

    def start(self, ins, outs, sems):
        _, s = place()
        _, n = counts()
        pltpu.make_async_copy(ins[0], outs[0].at[s], sems[2].at[0]).start()
        for way in (0, 1):
            follows = (s < n - 1) if way == 0 else (s > 0)

            @pl.when(follows)
            def _():
                self.hand_on(ins, outs, sems, way, 0).start()

    def step(self, ins, outs, sems, k):
        dp, s = place()
        _, n = counts()
        for way in (0, 1):
            sign = 1 - 2 * way
            follows = (s < n - 1) if way == 0 else (s > 0)

            @pl.when(self.guard(way, k))
            def _():
                block = outs[0].at[s - sign * k]
                remote(
                    block, block, sems[0].at[way, k - 1], sems[1].at[way, k - 1], (dp, s - sign)
                ).wait_recv()
                if k < n - 1:

                    @pl.when(follows)
                    def _():
                        self.hand_on(ins, outs, sems, way, k).start()

    def close(self, ins, outs, sems):
        _, s = place()
        _, n = counts()
        for way in (0, 1):
            follows = (s < n - 1) if way == 0 else (s > 0)
            for k in range(n - 1):

                @pl.when(jnp.logical_and(follows, self.guard(way, k)))
                def _():
                    self.hand_on(ins, outs, sems, way, k).wait_send()

        pltpu.make_async_copy(ins[0], outs[0].at[s], sems[2].at[0]).wait()

    def finish(self, ins, outs, sems):
        _, n = counts()
        for k in range(1, n):
            self.step(ins, outs, sems, k)
        self.close(ins, outs, sems)


def run(number, greet, *tasks):
    spans = []
    a = b = c = 0
    for task in tasks:
        spans.append((a, b, c))
        a += len(task.operands)
        b += len(task.outs)
        c += len(task.sems)
    n_in, n_out = a, b

    def kernel(*refs):
        ins, outs, sems = refs[:n_in], refs[n_in : n_in + n_out], refs[n_in + n_out :]
        greet()
        views = [
            (
                ins[i : i + len(t.operands)],
                outs[o : o + len(t.outs)],
                sems[m : m + len(t.sems)],
            )
            for t, (i, o, m) in zip(tasks, spans)
        ]
        for t, view in zip(tasks, views):
            t.start(*view)
        for t, view in zip(tasks, views):
            t.finish(*view)

    return pl.pallas_call(
        kernel,
        out_shape=[jax.ShapeDtypeStruct(o.shape, o.dtype) for t in tasks for o in t.outs],
        in_specs=[pl.BlockSpec(memory_space=pl.ANY)] * n_in,
        out_specs=[pl.BlockSpec(memory_space=pl.ANY)] * n_out,
        scratch_shapes=[s for t in tasks for s in t.sems],
        compiler_params=pltpu.CompilerParams(collective_id=number, has_side_effects=True),
    )(*[v for t in tasks for v in t.operands])


def gather_inputs(block_input, pack, fc_pack, out_rows):
    dpc, n = counts()
    tokens = Line(block_input)
    spread_out, spread_pack = Spread(out_rows), Spread(pack)

    def kernel(
        x_in, pack_in, fc_in, out_in, x_all, pack_all, fc_all, out_all, pack_mid, out_mid,
        x_send, x_recv, x_own, turn_send, turn_recv, local,
        z_send, z_recv, f_send, f_recv, *spreads
    ):
        dp, s = place()
        greet_all()
        rank = dp * n + s
        to_dp, to_s = rank % dpc, rank // dpc
        home = jnp.logical_and(to_dp == dp, to_s == s)
        turn = remote(out_in, out_mid, turn_send.at[0], turn_recv.at[0], (to_dp, to_s))
        keep_out = pltpu.make_async_copy(out_in, out_mid, local.at[0])
        keep_pack = pltpu.make_async_copy(pack_in.at[s], pack_mid.at[s], local.at[1])
        keep_fc = pltpu.make_async_copy(fc_in.at[s], fc_all.at[s], local.at[2])

        def shuffle(source, target, send, recv):
            return [
                remote(
                    source.at[(s + k) % n], target.at[s], send.at[k], recv.at[k], (dp, (s + k) % n)
                )
                for k in range(n - 1, 0, -1)
            ]

        keep_pack.start()
        for copy in shuffle(pack_in, pack_mid, z_send, z_recv):
            copy.start()

        @pl.when(home)
        def _():
            keep_out.start()

        @pl.when(jnp.logical_not(home))
        def _():
            turn.start()

        token_view = ((x_in,), (x_all,), (x_send, x_recv, x_own))
        out_view = ((out_mid,), (out_all,), spreads[:5])
        pack_view = ((pack_mid,), (pack_all,), spreads[5:])
        tokens.start(*token_view)

        @pl.when(home)
        def _():
            keep_out.wait()

        @pl.when(jnp.logical_not(home))
        def _():
            turn.wait()

        spread_out.start(*out_view)
        keep_pack.wait()
        for copy in shuffle(pack_in, pack_mid, z_send, z_recv):
            copy.wait()
        spread_pack.start(*pack_view)
        tokens.step(*token_view, 1)
        keep_fc.start()
        for copy in shuffle(fc_in, fc_all, f_send, f_recv):
            copy.start()
        for k in range(2, n - 1):
            tokens.step(*token_view, k)
        spread_out.middle(*out_view)
        spread_pack.middle(*pack_view)
        if n > 2:
            tokens.step(*token_view, n - 1)
        spread_out.close(*out_view)
        spread_pack.close(*pack_view)
        tokens.close(*token_view)
        keep_fc.wait()
        for copy in shuffle(fc_in, fc_all, f_send, f_recv):
            copy.wait()

    def grown(value, *lead):
        return jax.ShapeDtypeStruct(lead + value.shape, value.dtype)

    return pl.pallas_call(
        kernel,
        out_shape=[
            grown(block_input, n), grown(pack, dpc), grown(fc_pack), grown(out_rows, dpc),
            grown(pack), grown(out_rows),
        ],
        in_specs=[pl.BlockSpec(memory_space=pl.ANY)] * 4,
        out_specs=[pl.BlockSpec(memory_space=pl.ANY)] * 6,
        scratch_shapes=[
            *tokens.sems, dma(1), dma(1), dma(3),
            dma(n), dma(n), dma(n), dma(n), *spread_out.sems, *spread_pack.sems,
        ],
        compiler_params=pltpu.CompilerParams(collective_id=0, has_side_effects=True),
    )(block_input, pack, fc_pack, out_rows)[:4]


def shifted(value, by):
    _, n = counts()
    return lax.ppermute(value, "seq", [(i, (i + by) % n) for i in range(n)])


def total(own, received, mine):
    picked = [
        jnp.where(k == mine, widened(own[k]), widened(received[k])) for k in range(own.shape[0])
    ]
    result = picked[0]
    for value in picked[1:]:
        result = result + value
    return result


def fill(own, received, mine):
    slots = lax.broadcasted_iota(jnp.int32, (own.shape[0],) + (1,) * (own.ndim - 1), 0)
    return jnp.where(slots == mine, own, received)


def local(
    block_input,
    cotangent,
    ln1_gain,
    ln1_bias,
    qkv_weight,
    qv_bias,
    out_weight,
    out_bias,
    ln2_gain,
    ln2_bias,
    fc_weight,
    fc_bias,
    proj_weight,
    proj_bias,
):
    dp, s = place()
    dpc, n = counts()
    nc, ranks = dpc // 2, dpc * n
    core, chip = dp % 2, dp // 2
    tok_rows = block_input.shape[0]
    rows = qkv_weight.shape[0]
    units = fc_bias.shape[0]
    heads = H // n
    wide = heads * HD
    length = n * tok_rows
    score_scale = HD ** (-0.5)

    fields = (ln1_gain, ln1_bias, out_bias, ln2_gain, ln2_bias, proj_bias, qv_bias, fc_bias)
    span = -(-max(v.shape[0] for v in fields) // 128) * 128
    lines = -(-len(fields) // rows) * rows
    margin = lines // rows * span
    block = jnp.concatenate([jnp.pad(v[None], ((0, 0), (0, span - v.shape[0]))) for v in fields])
    block = jnp.pad(block, ((0, lines - len(fields)), (0, 0))).reshape(rows, margin)
    pack = jnp.concatenate(
        [
            qkv_weight.reshape(rows, 3, n, wide).transpose(2, 0, 1, 3).reshape(n, rows, 3 * wide),
            jnp.broadcast_to(block[None], (n, rows, margin)),
        ],
        axis=2,
    )
    fc_pack = fc_weight.reshape(rows, dpc, n, units).transpose(2, 0, 1, 3).reshape(n, rows, dpc * units)
    x_all, pack_all, fc_plane, out_all = gather_inputs(block_input, pack, fc_pack, out_weight)
    x_all, grad_half = lax.optimization_barrier((x_all, cotangent))
    grad_all = lax.dynamic_update_index_in_dim(
        jnp.zeros((n,) + grad_half.shape, grad_half.dtype), grad_half, s, 0
    )
    for k in range(1, n):
        grad_all = lax.dynamic_update_index_in_dim(grad_all, shifted(grad_half, k), (s - k + n) % n, 0)
    grad_seq = grad_all.reshape(length, D)
    stream_seq = widened(x_all.reshape(length, D))
    pack_rows = pack_all.reshape(D, pack.shape[2])
    qkv_cols = pack_rows[:, : 3 * wide]
    out_rows = out_all.reshape(wide, D)
    smalls = pack_rows[:, 3 * wide :].reshape(ranks, lines, span)
    gain_one, bias_one, out_bias_full, gain_two, bias_two, proj_bias_full = (
        widened(smalls[:, i, :rows].reshape(D)) for i in range(6)
    )
    qv_full = smalls[:, 6, : qv_bias.shape[0]].reshape(2, n, wide)
    qv_own = widened(lax.dynamic_index_in_dim(qv_full, s, 1, keepdims=False))
    fc_bias_cols = widened(
        lax.dynamic_index_in_dim(
            smalls[:, 7, :units].reshape(dpc, n, units), s, 1, keepdims=False
        ).reshape(dpc * units)
    )

    normed_one = halved(layer_norm(stream_seq, gain_one, bias_one))
    projected = matmul(normed_one, qkv_cols)

    def by_head(values):
        return values.reshape(length, heads, HD).transpose(1, 0, 2)

    def by_token(values):
        return values.transpose(1, 0, 2).reshape(length, wide)

    queries = by_head(halved(projected[:, :wide] + qv_own[0]))
    keys = by_head(halved(projected[:, wide : 2 * wide]))
    values = by_head(halved(projected[:, 2 * wide :] + qv_own[1]))
    position = jnp.arange(length, dtype=jnp.int32)
    visible = position[None, :] <= position[:, None]
    scores = (
        jnp.einsum("hqd,hkd->hqk", queries, keys, preferred_element_type=jnp.float32) * score_scale
    )
    log_total = jnp.log(
        jnp.sum(jnp.where(visible, jnp.exp(scores), 0.0), axis=-1, keepdims=True)
    )
    probs = jnp.where(visible, jnp.exp(scores - log_total), 0.0)
    shares = halved(probs)
    attended_heads = halved(
        jnp.einsum("hqk,hkd->hqd", shares, values, preferred_element_type=jnp.float32)
    )
    attended = by_token(attended_heads)
    mixed = halved(matmul(attended, out_rows)).reshape(n, tok_rows, D)
    mixed_got, fc_all = run(1, greet_near, Exchange(mixed), Spread(fc_plane))
    fc_cols = fc_all.reshape(D, dpc * units)
    stream = widened(block_input)
    middle = stream + total(mixed, mixed_got, s) + out_bias_full
    normed_two = halved(layer_norm(middle, gain_two, bias_two))
    normed_all, proj_all = run(2, greet_near, Line(normed_two), Spread(proj_weight))
    proj_rows = proj_all.reshape(dpc * units, D)
    normed_seq = normed_all.reshape(length, D)
    grad_out = widened(cotangent)
    d_proj_bias = jnp.sum(grad_out, axis=0)
    pre_act = matmul(normed_seq, fc_cols) + fc_bias_cols
    hidden = halved(gelu_tanh(pre_act))
    grad_hidden = matmul(grad_seq, proj_rows.T)
    _, gelu_back = jax.vjp(gelu_tanh, pre_act)
    grad_pre = gelu_back(grad_hidden)[0]
    pre_half = halved(grad_pre)
    back_two = halved(matmul(pre_half, fc_cols.T)).reshape(n, tok_rows, D)
    (back_two_got,) = run(3, greet_seq, Exchange(back_two))
    ff_part = halved(matmul(hidden, proj_rows)).reshape(n, tok_rows, D)

    def by_core(values):
        return halved(values).reshape(nc, 2, -1, values.shape[-1])

    d_proj = by_core(matmul(hidden.T, grad_seq))
    d_fc = by_core(matmul(normed_seq.T, pre_half))
    d_fc_bias = jnp.sum(grad_pre, axis=0).reshape(dpc, 1, units)
    _, norm_back_two = jax.vjp(layer_norm, middle, gain_two, bias_two)
    mid_branch, d_ln2_gain, d_ln2_bias = norm_back_two(total(back_two, back_two_got, s))
    grad_middle = grad_out + mid_branch
    d_out_bias = jnp.sum(grad_middle, axis=0)
    middle_all, d_proj_got, d_fc_got = run(
        4, greet_near, Line(halved(grad_middle)), Partner(d_proj), Partner(d_fc)
    )

    def pair(own, received):
        kept = lax.dynamic_index_in_dim(own, core, 1, keepdims=False)
        return halved(widened(kept) + widened(received))

    middle_all, ff_part = lax.optimization_barrier((middle_all, ff_part))
    ff_sum = widened(lax.dynamic_index_in_dim(ff_part, s, 0, keepdims=False))
    for k in range(1, n):
        slot = lax.dynamic_index_in_dim(ff_part, (s + k) % n, 0, keepdims=False)
        ff_sum = ff_sum + widened(shifted(slot, k))
    d_proj, d_fc = pair(d_proj, d_proj_got), pair(d_fc, d_fc_got)
    middle_half = middle_all.reshape(length, D)
    d_out = by_core(matmul(attended.T, middle_half))
    grad_attended = matmul(middle_half, out_rows.T)
    grad_att = by_head(halved(grad_attended))
    row_delta = jnp.sum(by_head(grad_attended) * widened(attended_heads), axis=-1, keepdims=True)
    grad_shares = jnp.einsum("hqd,hkd->hqk", grad_att, values, preferred_element_type=jnp.float32)
    grad_scores = halved(probs * (grad_shares - row_delta))
    grad_q = (
        jnp.einsum("hqk,hkd->hqd", grad_scores, keys, preferred_element_type=jnp.float32)
        * score_scale
    )
    grad_k = (
        jnp.einsum("hqk,hqd->hkd", grad_scores, queries, preferred_element_type=jnp.float32)
        * score_scale
    )
    grad_v = jnp.einsum("hqk,hqd->hkd", shares, grad_att, preferred_element_type=jnp.float32)
    grad_qkv = jnp.concatenate([by_token(grad_q), by_token(grad_k), by_token(grad_v)], axis=1)
    qkv_half = halved(grad_qkv)
    back_one = halved(matmul(qkv_half, qkv_cols.T)).reshape(n, tok_rows, D)
    d_qkv = by_core(matmul(normed_one.T, qkv_half))
    sums = jnp.sum(grad_qkv, axis=0)
    d_qv = jnp.stack([sums[:wide], sums[2 * wide :]])[:, None]
    back_one_got, d_proj_parts, d_fc_parts, d_qkv_got, d_out_got = run(
        5, greet_near, Exchange(back_one), Plane(d_proj), Plane(d_fc), Partner(d_qkv), Partner(d_out)
    )
    proj_grad = total(d_proj, d_proj_parts, chip)
    fc_rows = halved(total(d_fc, d_fc_parts, chip)).reshape(n, rows, dpc * units)
    d_qkv, d_out = pair(d_qkv, d_qkv_got), pair(d_out, d_out_got)
    _, norm_back_one = jax.vjp(layer_norm, stream, gain_one, bias_one)
    stream_branch, d_ln1_gain, d_ln1_bias = norm_back_one(total(back_one, back_one_got, s))
    grad_stream = grad_middle + stream_branch
    turn = jnp.arange(n, dtype=jnp.int32)[None, :, None] == s
    vectors = jnp.concatenate(
        [
            v.reshape(ranks, rows)
            for v in (d_ln1_gain, d_ln1_bias, d_out_bias, d_ln2_gain, d_ln2_bias, d_proj_bias)
        ]
        + [
            jnp.where(turn, d_qv, 0.0).reshape(ranks, -1),
            jnp.where(turn, d_fc_bias, 0.0).reshape(ranks, units),
        ],
        axis=1,
    )
    used = vectors.shape[1]
    vectors = jnp.pad(vectors, ((0, 0), (0, -used % 128))).reshape(ranks, -1, 128)
    d_qkv = d_qkv.reshape(nc, n, rows, 3 * wide)
    d_qkv_parts, d_out_parts, fc_got, vectors_got = run(
        6, greet_all, Owners(d_qkv), Blocks(d_out), Exchange(fc_rows), Everyone(vectors)
    )
    output = middle + ff_sum + proj_bias_full
    fc_grad = (
        widened(fill(fc_rows, fc_got, s))
        .reshape(n, rows, dpc, units)
        .transpose(1, 2, 0, 3)
        .reshape(rows, FF)
    )
    vector = jnp.sum(fill(vectors, vectors_got, dp * n + s), axis=0).reshape(-1)
    firsts = [vector[i * rows : (i + 1) * rows] for i in range(6)]
    at = 6 * rows
    qv_grad = vector[at : at + qv_bias.shape[0]]
    at += qv_bias.shape[0]
    fc_bias_grad = vector[at : at + units]
    qkv_grad = (
        jnp.sum(widened(d_qkv_parts), axis=0)
        .reshape(n, rows, 3, wide)
        .transpose(1, 2, 0, 3)
        .reshape(rows, 3 * D)
    )
    out_grad = jnp.sum(widened(d_out_parts), axis=0)
    return (
        output,
        grad_stream,
        firsts[0],
        firsts[1],
        qkv_grad,
        qv_grad,
        out_grad,
        firsts[2],
        firsts[3],
        firsts[4],
        fc_grad,
        fc_bias_grad,
        proj_grad,
        firsts[5],
    )


def solution(mesh):
    in_specs = (
        P(("dp", "seq"), None),
        P(("dp", "seq"), None),
        P(("dp", "seq")),
        P(("dp", "seq")),
        P(("dp", "seq"), None),
        P(("dp", "seq")),
        P(("dp", "seq"), None),
        P(("dp", "seq")),
        P(("dp", "seq")),
        P(("dp", "seq")),
        P(("dp", "seq"), None),
        P(("dp", "seq")),
        P(("dp", "seq"), None),
        P(("dp", "seq")),
    )
    out_specs = (
        P(("dp", "seq"), None),
        P(("dp", "seq"), None),
        P(("dp", "seq")),
        P(("dp", "seq")),
        P(("dp", "seq"), None),
        P(("dp", "seq")),
        P(("dp", "seq"), None),
        P(("dp", "seq")),
        P(("dp", "seq")),
        P(("dp", "seq")),
        P(("dp", "seq"), None),
        P(("dp", "seq")),
        P(("dp", "seq"), None),
        P(("dp", "seq")),
    )
    return jax.shard_map(local, mesh=mesh, in_specs=in_specs, out_specs=out_specs, check_vma=False)
```
